256 devices in a mesh: users: 16 (over x_hi, z), items: 16 (over x_lo, y, core).
Axes of the slice: x: 4 (x_hi: 2, x_lo: 2; x = x_hi * 2 + x_lo), y: 4, z: 8, core: 2. Of those that a mesh axis runs over, the one named last changes fastest.
Arguments:
- logs: bfloat16 [256, 16, 512, 512], P('users', 'items'), may hold values from -6 to 6
- tile_rows: int32 [256, 16, 512], P('users', 'items'), may hold values from 0 to 1, as said below
- slot_owner: int32 [256, 16], P('users', 'items'), may hold values from 0 to 15, as said below
- counts: int32 [16, 16], P('users', 'items'), may hold values from 0 to 16, as said below
- owner_source: int32 [16, 16, 8], P('users', 'items'), may hold values from 0 to 15, as said below
- user_factors: bfloat16 [16, 16, 512, 512], P('users', 'items'), may hold values from -1.26134462 to 1.26134462
- item_factors: bfloat16 [16, 16, 512, 512], P('users', 'items'), may hold values from -1.26134462 to 1.26134462
Outputs:
- users_out: bfloat16 [16, 16, 512, 512], P('users', 'items')
- items_out: bfloat16 [16, 16, 512, 512], P('users', 'items')
The draws below stay inside these ranges and needn't reach their ends.
Inputs may be any that keep to these rules, and one draw needn't show every extreme that they name: `slot_owner`: among the first counts slots of a source each owner appears at most once, and owner u has a slot at source s in column i exactly when s is listed in owner_source[u, i]; slots from counts on hold no tile. `counts`: in every column some source holds 16 tiles. `owner_source`: the 8 sources listed for one owner are distinct. `tile_rows`: every slot has exactly 256 rows equal to 1.
All inputs are finite; a program needn't handle non-finite values.
Results may differ from the reference program's by a relative error of at most 0.0095.
Values may be sent and summed in bfloat16 or wider, within the bound.
No kernel may reach another device: no remote copies, remote signals or barrier semaphores. Data moves between devices by JAX's collectives and lax.ppermute only.
A program may use at most 128 MiB of HBM per device.

```python
import jax
import jax.numpy as jnp
from jax import lax

RANK = 512
TILE = 512
STRATA = 8
LOG = 16
CYCLE = 16
LIVE = 256


def column_lists(column_key):
    key_weight, key_hot, key_noise, key_shuffle, key_filler = jax.random.split(column_key, 5)
    slot_lane = jnp.arange(LOG, dtype=jnp.int32)
    weights = jax.random.randint(key_weight, (LOG,), 0, 3).astype(jnp.int32)
    hottest = jax.random.randint(key_hot, (), 0, LOG).astype(jnp.int32)
    weights = jnp.where(slot_lane == hottest, 4, weights)
    noise = jax.vmap(lambda sub: jax.random.permutation(sub, LOG))(jax.random.split(key_noise, LOG)).astype(jnp.int32)
    scores = weights[None, :] * LOG + noise
    chosen = lax.top_k(scores, STRATA)[1].astype(jnp.int32)
    shuffle = jax.vmap(lambda sub: jax.random.permutation(sub, STRATA))(jax.random.split(key_shuffle, LOG)).astype(jnp.int32)
    sources = jnp.take_along_axis(chosen, shuffle, axis=1)
    picked = jnp.any(chosen[:, :, None] == slot_lane[None, None, :], axis=1)
    chosen_by = picked.T.astype(jnp.int32)
    filled = jnp.sum(chosen_by, axis=1).astype(jnp.int32)
    ranked = jnp.argsort(1 - chosen_by, axis=1, stable=True).astype(jnp.int32)
    filler = jax.random.randint(key_filler, (LOG, LOG), 0, LOG).astype(jnp.int32)
    owners = jnp.where(slot_lane[None, :] < filled[:, None], ranked, filler)
    return (sources, owners.reshape(LOG * LOG), filled)


def all_lists(key):
    keys = jax.random.split(jax.random.fold_in(key, 7), CYCLE)
    return jax.vmap(column_lists)(keys)


def draw_owner_source(key, part):
    return jnp.transpose(all_lists(key)[0], (1, 0, 2)).astype(jnp.int32)


def draw_slot_owner(key, part):
    return all_lists(key)[1].T.astype(jnp.int32)


def draw_counts(key, part):
    return all_lists(key)[2].T.astype(jnp.int32)


def draw_tile_rows(key, part):
    keys = jax.random.split(jax.random.fold_in(key, 11), LOG * LOG * CYCLE)
    shuffled = jax.vmap(lambda sub: jax.random.permutation(sub, TILE))(keys)
    marks = (shuffled < LIVE).astype(jnp.int32)
    return marks.reshape(LOG * LOG, CYCLE, TILE)


def scaled_field(key, shape, spread, bound):
    key_value = jax.random.fold_in(key, 0)
    values = jax.random.normal(key_value, shape, jnp.float32)
    return jnp.clip(values * spread, -bound, bound)


def draw_logs(key, part):
    field = scaled_field(jax.random.fold_in(key, 21), (LOG * LOG, CYCLE, TILE, TILE), 1.0, 6.0)
    return field.astype(jnp.bfloat16)


def draw_user_factors(key, part):
    spread = RANK ** (-0.25)
    field = scaled_field(jax.random.fold_in(key, 23), (LOG, CYCLE, TILE, RANK), spread, 6.0 * spread)
    return field.astype(jnp.bfloat16)


def draw_item_factors(key, part):
    spread = RANK ** (-0.25)
    field = scaled_field(jax.random.fold_in(key, 29), (LOG, CYCLE, TILE, RANK), spread, 6.0 * spread)
    return field.astype(jnp.bfloat16)


def setup_inputs(seed: int = 0) -> dict:
    splits = jax.random.split(jax.random.key(seed), 8)
    return {
        "logs": draw_logs(jax.random.fold_in(splits[7], 71), 0),
        "tile_rows": draw_tile_rows(jax.random.fold_in(splits[7], 71), 0),
        "slot_owner": draw_slot_owner(jax.random.fold_in(splits[7], 71), 0),
        "counts": draw_counts(jax.random.fold_in(splits[7], 71), 0),
        "owner_source": draw_owner_source(jax.random.fold_in(splits[7], 71), 0),
        "user_factors": draw_user_factors(jax.random.fold_in(splits[7], 71), 0),
        "item_factors": draw_item_factors(jax.random.fold_in(splits[7], 71), 0),
    }


learn_rate = 0.01
shrink_rate = 0.05


def reference(logs, tile_rows, slot_owner, counts, owner_source, user_factors, item_factors):
    slot_lane = jnp.arange(LOG, dtype=jnp.int32)
    column = jnp.arange(CYCLE, dtype=jnp.int32)
    owners_slot = slot_owner.reshape(LOG, LOG, CYCLE)
    filled = slot_lane[None, :, None] < counts[:, None, :]
    matches = (owners_slot[:, :, None, :] == slot_lane[None, None, :, None]) & filled[:, :, None, :]
    slot_of = jnp.argmax(matches, axis=1).astype(jnp.int32)
    users_now = user_factors
    items_now = item_factors
    for stratum in range(STRATA):
        source = owner_source[:, :, stratum]
        slot_pick = slot_of[source, slot_lane[:, None], column[None, :]]
        log_row = (source * LOG + slot_pick).astype(jnp.int32)
        ratings = logs[log_row, column[None, :]].astype(jnp.float32)
        row_mask = tile_rows[log_row, column[None, :]].astype(jnp.float32)
        users_wide = users_now.astype(jnp.float32)
        items_wide = jnp.roll(items_now, stratum, axis=1).astype(jnp.float32)
        predicted = jnp.einsum('abnr,abmr->abnm', users_wide, items_wide)
        residual = (row_mask[..., None] * (ratings - predicted)).astype(jnp.bfloat16)
        resid_wide = residual.astype(jnp.float32)
        user_grad = jnp.einsum('abnm,abmr->abnr', resid_wide, items_wide)
        item_grad = jnp.einsum('abnm,abnr->abmr', resid_wide, users_wide)
        users_now = (users_wide + learn_rate * (user_grad - shrink_rate * users_wide)).astype(jnp.bfloat16)
        items_new = (items_wide + learn_rate * (item_grad - shrink_rate * items_wide)).astype(jnp.bfloat16)
        items_now = jnp.roll(items_new, -stratum, axis=1)
    return users_now, items_now
```

```python
import jax
import jax.numpy as jnp
from jax import lax
from jax.experimental import pallas as pl
from jax.experimental.pallas import tpu as pltpu
from jax.sharding import PartitionSpec as P


learn_rate = 0.01
shrink_rate = 0.05

LANES = 128
LIVE = 256
CHUNKS = 4
GROUPS = ((1, 15, 8), (2, 14, 7, 9), (3, 13, 6, 10), (4, 12, 5, 11, 0))

F32 = jnp.float32
BF16 = jnp.bfloat16


def slot_for(owner, slot_owner, count, slots):
    found = jnp.int32(0)
    for slot in range(slots - 1, -1, -1):
        hit = (slot_owner[slot] == owner) & (slot < count)
        found = jnp.where(hit, jnp.int32(slot), found)
    return found


def dot(a, b, ca, cb):
    return lax.dot_general(a, b, (((ca,), (cb,)), ((), ())), preferred_element_type=F32)


def one_hot_rows(code, rows):
    lane_code = jnp.broadcast_to(code, (rows, code.shape[1]))
    row = lax.broadcasted_iota(jnp.int32, lane_code.shape, 0).astype(F32)
    return jnp.where(lane_code == row, 1.0, 0.0).astype(BF16)


def compact_kernel(group, slots, meta_ref, *refs):
    tiles = refs[: len(group)]
    marks_ref = refs[len(group)]
    outs = refs[len(group) + 1 :]
    width = marks_ref.shape[2]
    blocks = width // LANES
    below = lax.broadcasted_iota(jnp.int32, (width, width), 0)
    upto = lax.broadcasted_iota(jnp.int32, (width, width), 1)
    ramp = jnp.where(below <= upto, 1.0, 0.0).astype(BF16)
    me = meta_ref[slots + 1]
    for place, shift in enumerate(group):
        slot = slot_for(lax.rem(me + shift, slots), meta_ref, meta_ref[slots], slots)
        marks = marks_ref[slot].astype(F32)
        marks8 = jnp.broadcast_to(marks, (8, width))
        order = dot(marks8.astype(BF16), ramp, 1, 0)
        code8 = jnp.where(marks8 > 0.5, order - 1.0, -1.0)
        select = one_hot_rows(code8[0:1], LIVE)
        packed = dot(select, tiles[place][0, 0], 1, 0).astype(BF16)
        sub = lax.broadcasted_iota(jnp.int32, (8, LANES), 0)
        tail = jnp.zeros((8, LANES), F32)
        for b in range(blocks):
            lanes = slice(b * LANES, (b + 1) * LANES)
            outs[place][b * LIVE : (b + 1) * LIVE, :] = packed[:, lanes]
            tail = jnp.where(sub == b, code8[:, lanes], tail)
        outs[place][blocks * LIVE :, :] = tail.astype(BF16)


def compact(logs, row_marks, meta, group, slots):
    width = logs.shape[2]
    rows = (width // LANES) * LIVE + 8

    def tile_map(shift):
        def index(step, meta_ref):
            owner = lax.rem(meta_ref[slots + 1] + shift, slots)
            return (slot_for(owner, meta_ref, meta_ref[slots], slots), 0, 0, 0)

        return index

    return pl.pallas_call(
        lambda *refs: compact_kernel(group, slots, *refs),
        out_shape=[jax.ShapeDtypeStruct((rows, LANES), BF16) for _ in group],
        grid_spec=pltpu.PrefetchScalarGridSpec(
            num_scalar_prefetch=1,
            grid=(1,),
            in_specs=[pl.BlockSpec((1, 1, width, width), tile_map(shift)) for shift in group]
            + [pl.BlockSpec(row_marks.shape, lambda step, meta_ref: (0, 0, 0))],
            out_specs=[pl.BlockSpec((rows, LANES), lambda step, meta_ref: (0, 0)) for _ in group],
        ),
        cost_estimate=pl.CostEstimate(
            flops=len(group) * 2 * LIVE * width * width,
            bytes_accessed=len(group) * 3 * width * width,
            transcendentals=0,
        ),
        name="compact",
    )(meta, *([logs] * len(group)), row_marks)


def stage_kernel(shifts, slots, strata, meta_ref, *refs):
    blocks = refs[: len(shifts)]
    out_ref = refs[len(shifts)]
    sem = refs[len(shifts) + 1]
    me = meta_ref[strata]
    for s in range(strata):
        shift = lax.rem(me - meta_ref[s] + slots, slots)
        for place, d in enumerate(shifts):

            @pl.when(shift == d)
            def _():
                pltpu.make_async_copy(blocks[place], out_ref.at[s], sem.at[s]).start()

    for s in range(strata):
        pltpu.make_async_copy(blocks[0], out_ref.at[s], sem.at[s]).wait()


def stage(blocks, shifts, meta, slots, strata):
    rows, lanes = blocks[0].shape
    return pl.pallas_call(
        lambda *refs: stage_kernel(shifts, slots, strata, *refs),
        out_shape=jax.ShapeDtypeStruct((strata, rows, lanes), BF16),
        in_specs=[pl.BlockSpec(memory_space=pltpu.SMEM)]
        + [pl.BlockSpec(memory_space=pl.ANY)] * len(blocks),
        out_specs=pl.BlockSpec(memory_space=pltpu.VMEM),
        scratch_shapes=[pltpu.SemaphoreType.DMA((strata,))],
        name="stage",
    )(meta, *blocks)


def code_row(code_ref, blocks):
    code = code_ref[0].astype(F32)
    return jnp.concatenate([code[b : b + 1] for b in range(blocks)], axis=1)


def chunk_step(users_live, ratings, items_old):
    predicted = dot(users_live, items_old, 1, 1)
    residual = (ratings.astype(F32) - predicted).astype(BF16)
    item_grad = dot(residual, users_live, 0, 0)
    wide = items_old.astype(F32)
    items_new = wide + learn_rate * (item_grad - shrink_rate * wide)
    return residual, items_new.astype(BF16)


def finish_users(users_old, residuals, items_old, code_ref):
    blocks = users_old.shape[0] // LANES
    select = one_hot_rows(code_row(code_ref, blocks), LIVE)
    residual = jnp.concatenate([r[...] for r in residuals], axis=1)
    spread = dot(select, residual, 0, 0).astype(BF16)
    grad = None
    step = spread.shape[1] // len(items_old)
    for k, chunk in enumerate(items_old):
        part = dot(spread[:, k * step : (k + 1) * step], chunk[...], 1, 0)
        grad = part if grad is None else grad + part
    wide = users_old.astype(F32)
    return (wide + learn_rate * (grad - shrink_rate * wide)).astype(BF16)


def ratings_of(rating_refs):
    return jnp.concatenate([r[0] for r in rating_refs], axis=1)


def first_kernel(begin, chunks, per, *refs):
    refs = list(refs)
    users_ref = refs.pop(0)
    residuals = [] if begin else [refs.pop(0) for _ in range(chunks)]
    items_before = [] if begin else [refs.pop(0) for _ in range(chunks)]
    code_before = None if begin else refs.pop(0)
    code_now = refs.pop(0)
    rating_refs = [refs.pop(0) for _ in range(per)]
    items_ref = refs.pop(0)
    if begin:
        live_ref, residual_ref, out_ref = refs
        users = users_ref[...]
    else:
        live_ref, residual_ref, out_ref, users_out = refs
        users = finish_users(users_ref[...], residuals, items_before, code_before)
        users_out[...] = users
    select = one_hot_rows(code_row(code_now, users.shape[0] // LANES), LIVE)
    live = dot(select, users, 1, 0).astype(BF16)
    live_ref[...] = live
    residual, items_new = chunk_step(live, ratings_of(rating_refs), items_ref[...])
    residual_ref[...] = residual
    out_ref[...] = items_new


def next_kernel(per, live_ref, *refs):
    rating_refs = refs[:per]
    items_ref, residual_ref, out_ref = refs[per:]
    residual, items_new = chunk_step(live_ref[...], ratings_of(rating_refs), items_ref[...])
    residual_ref[...] = residual
    out_ref[...] = items_new


def last_kernel(chunks, users_ref, *refs):
    residuals = refs[:chunks]
    items_before = refs[chunks : 2 * chunks]
    code_ref, out_ref = refs[2 * chunks :]
    out_ref[...] = finish_users(users_ref[...], residuals, items_before, code_ref)


def whole(array):
    return pl.BlockSpec(array.shape, lambda step: (0,) * array.ndim)


def code_spec(staged, stratum):
    last = staged.shape[1] // 8 - 1
    return pl.BlockSpec((1, 8, LANES), lambda step: (stratum, last, 0))


def rating_specs(stratum, chunk, per):
    return [
        pl.BlockSpec((1, LIVE, LANES), lambda step, b=chunk * per + b: (stratum, b, 0))
        for b in range(per)
    ]


def run(kernel, operands, specs, outs, flops, name):
    moved = sum(x.size * x.dtype.itemsize for x in outs) * 2
    return pl.pallas_call(
        kernel,
        out_shape=outs,
        grid=(1,),
        in_specs=specs,
        out_specs=[whole(x) for x in outs],
        cost_estimate=pl.CostEstimate(flops=flops, bytes_accessed=moved, transcendentals=0),
        name=name,
    )(*operands)


def passed_along(array, axis, by):
    peers = lax.axis_size(axis)
    return lax.ppermute(array, axis, [(i, (i + by) % peers) for i in range(peers)])


def local(logs, tile_rows, slot_owner, counts, owner_source, user_factors, item_factors):
    slots = logs.shape[0]
    strata = owner_source.shape[2]
    me = lax.axis_index("users").astype(jnp.int32)
    meta_out = jnp.concatenate([slot_owner[:, 0], counts[0], me[None]])
    meta_in = jnp.concatenate([owner_source[0, 0], me[None]])

    arrived, shifts = [], []
    for group in GROUPS:
        packed = compact(logs, tile_rows, meta_out, group, slots)
        for shift, block in zip(group, packed):
            shifts.append(shift)
            arrived.append(passed_along(block, "users", shift) if shift else block)
    staged = stage(arrived, tuple(shifts), meta_in, slots, strata)

    users = user_factors[0, 0]
    rows, rank = users.shape
    size = rows // CHUNKS
    per = size // LANES
    items = [item_factors[0, 0, k * size : (k + 1) * size] for k in range(CHUNKS)]
    live_shape = jax.ShapeDtypeStruct((LIVE, rank), BF16)
    residual_shape = jax.ShapeDtypeStruct((LIVE, size), BF16)
    chunk_shape = jax.ShapeDtypeStruct((size, rank), BF16)
    users_shape = jax.ShapeDtypeStruct((rows, rank), BF16)
    chunk_flops = 4 * LIVE * size * rank
    users_flops = 2 * rows * rows * (LIVE + rank)

    residuals = live = None
    before = items
    for stratum in range(strata):
        outgoing, now = [], []
        for k in range(CHUNKS):
            ratings = [staged] * per
            spec_r = rating_specs(stratum, k, per)
            if k == 0:
                operands, specs = [users], [whole(users)]
                outs = [live_shape, residual_shape, chunk_shape]
                if stratum:
                    operands += residuals + before + [staged]
                    specs += [whole(x) for x in residuals + before]
                    specs += [code_spec(staged, stratum - 1)]
                    outs.append(users_shape)
                operands += [staged] + ratings + [items[k]]
                specs += [code_spec(staged, stratum)] + spec_r + [whole(items[k])]
                results = run(
                    lambda *refs, b=stratum == 0: first_kernel(b, CHUNKS, per, *refs),
                    operands,
                    specs,
                    outs,
                    chunk_flops + users_flops,
                    "first",
                )
                live = results[0]
                if stratum:
                    users = results[3]
                residual, moved = results[1], results[2]
            else:
                residual, moved = run(
                    lambda *refs: next_kernel(per, *refs),
                    [live] + ratings + [items[k]],
                    [whole(live)] + spec_r + [whole(items[k])],
                    [residual_shape, chunk_shape],
                    chunk_flops,
                    "next",
                )
            now.append(residual)
            by = 1 if stratum + 1 < strata else 1 - strata
            outgoing.append(passed_along(moved, "items", by))
        residuals, before, items = now, items, outgoing
    (users,) = run(
        lambda *refs: last_kernel(CHUNKS, *refs),
        [users] + residuals + before + [staged],
        [whole(x) for x in [users] + residuals + before] + [code_spec(staged, strata - 1)],
        [users_shape],
        users_flops,
        "last",
    )
    return (users[None, None], jnp.concatenate(items, axis=0)[None, None])


def solution(mesh):
    placed = (
        P("users", "items", None, None),
        P("users", "items", None),
        P("users", "items"),
        P("users", "items"),
        P("users", "items", None),
        P("users", "items", None, None),
        P("users", "items", None, None),
    )
    return jax.shard_map(
        local,
        mesh=mesh,
        in_specs=placed,
        out_specs=(P("users", "items", None, None), P("users", "items", None, None)),
        check_vma=False,
    )
```

```python
import functools

import jax
import jax.numpy as jnp
from jax import lax
from jax.experimental import pallas as pl
from jax.experimental.pallas import tpu as pltpu
from jax.sharding import PartitionSpec as P


learn_rate = 0.01
shrink_rate = 0.05

LANES = 128
LIVE = 256
VMEM_LIMIT = 16 * 1024 * 1024
CHUNKS = 4
GROUPS = ((3, 13), (5, 11, 4, 12), (2, 14, 6, 10), (1, 15, 7, 9, 8, 0))

F32 = jnp.float32
BF16 = jnp.bfloat16


def slot_for(owner, slot_owner, count, slots):
    found = jnp.int32(0)
    for slot in range(slots - 1, -1, -1):
        hit = (slot_owner[slot] == owner) & (slot < count)
        found = jnp.where(hit, jnp.int32(slot), found)
    return found


def dot(a, b, ca, cb):
    return lax.dot_general(a, b, (((ca,), (cb,)), ((), ())), preferred_element_type=F32)


def one_hot_rows(code, rows):
    lane_code = jnp.broadcast_to(code, (rows, code.shape[1]))
    row = lax.broadcasted_iota(jnp.int32, lane_code.shape, 0).astype(F32)
    return jnp.where(lane_code == row, 1.0, 0.0).astype(BF16)


def compact_kernel(group, slots, meta_ref, *refs):
    tiles = refs[: len(group)]
    marks_ref = refs[len(group)]
    outs = refs[len(group) + 1 : -1]
    select_ref = refs[-1]
    width = marks_ref.shape[2]
    blocks = width // LANES
    below = lax.broadcasted_iota(jnp.int32, (width, width), 0)
    upto = lax.broadcasted_iota(jnp.int32, (width, width), 1)
    ramp = jnp.where(below <= upto, 1.0, 0.0).astype(BF16)
    me = meta_ref[slots + 1]
    marks8 = []
    for shift in group:
        slot = slot_for(lax.rem(me + shift, slots), meta_ref, meta_ref[slots], slots)
        marks8.append(jnp.broadcast_to(marks_ref[slot].astype(F32), (8, width)))
    marks_all = jnp.concatenate(marks8, axis=0)
    order = dot(marks_all.astype(BF16), ramp, 1, 0)
    codes = jnp.where(marks_all > 0.5, order - 1.0, -1.0)
    band = 32
    row = lax.broadcasted_iota(jnp.int32, (band, width), 0).astype(F32)
    for place in range(len(group)):
        tile_ref, out_ref = tiles[place], outs[place]
        code8 = codes[place * 8 : (place + 1) * 8]
        code = jnp.broadcast_to(code8[0:1], (band, width))

        def fill(step, carry):
            hit = code == row + (step * band).astype(F32)
            start = pl.multiple_of(step * band, band)
            select_ref[pl.ds(start, band), :] = jnp.where(hit, 1.0, 0.0).astype(BF16)
            return carry

        lax.fori_loop(0, LIVE // band, fill, 0)

        def pack(block, carry):
            lane = pl.multiple_of(block * LANES, LANES)
            start = pl.multiple_of(block * LIVE, LIVE)
            part = dot(select_ref[...], tile_ref[0, 0, :, pl.ds(lane, LANES)], 1, 0)
            out_ref[pl.ds(start, LIVE), :] = part.astype(BF16)
            return carry

        lax.fori_loop(0, blocks, pack, 0)
        sub = lax.broadcasted_iota(jnp.int32, (8, LANES), 0)
        tail = jnp.zeros((8, LANES), F32)
        for b in range(blocks):
            tail = jnp.where(sub == b, code8[:, b * LANES : (b + 1) * LANES], tail)
        out_ref[blocks * LIVE :, :] = tail.astype(BF16)


def compact(logs, row_marks, meta, group, slots):
    width = logs.shape[2]
    rows = (width // LANES) * LIVE + 8

    def tile_map(shift):
        def index(step, meta_ref):
            owner = lax.rem(meta_ref[slots + 1] + shift, slots)
            return (slot_for(owner, meta_ref, meta_ref[slots], slots), 0, 0, 0)

        return index

    return pl.pallas_call(
        lambda *refs: compact_kernel(group, slots, *refs),
        out_shape=[jax.ShapeDtypeStruct((rows, LANES), BF16) for _ in group],
        grid_spec=pltpu.PrefetchScalarGridSpec(
            num_scalar_prefetch=1,
            grid=(1,),
            in_specs=[pl.BlockSpec((1, 1, width, width), tile_map(shift)) for shift in group]
            + [pl.BlockSpec(row_marks.shape, lambda step, meta_ref: (0, 0, 0))],
            out_specs=[pl.BlockSpec((rows, LANES), lambda step, meta_ref: (0, 0)) for _ in group],
            scratch_shapes=[pltpu.VMEM((LIVE, width), BF16)],
        ),
        cost_estimate=pl.CostEstimate(
            flops=len(group) * 2 * LIVE * width * width,
            bytes_accessed=len(group) * 3 * width * width,
            transcendentals=0,
        ),
        compiler_params=pltpu.CompilerParams(vmem_limit_bytes=VMEM_LIMIT),
        name="compact",
    )(meta, *([pltpu.with_memory_space_constraint(logs, pltpu.HBM)] * len(group)), row_marks)


def stage_kernel(shifts, slots, strata, meta_ref, *refs):
    blocks = refs[: len(shifts)]
    out_ref = refs[len(shifts)]
    sem = refs[len(shifts) + 1]
    me = meta_ref[strata]
    for s in range(strata):
        shift = lax.rem(me - meta_ref[s] + slots, slots)
        for place, d in enumerate(shifts):

            @pl.when(shift == d)
            def _():
                pltpu.make_async_copy(blocks[place], out_ref.at[s], sem.at[s]).start()

    for s in range(strata):
        pltpu.make_async_copy(blocks[0], out_ref.at[s], sem.at[s]).wait()


def stage(blocks, shifts, meta, slots, strata):
    rows, lanes = blocks[0].shape
    return pl.pallas_call(
        lambda *refs: stage_kernel(shifts, slots, strata, *refs),
        out_shape=pltpu.VMEM((strata, rows, lanes), BF16),
        in_specs=[pl.BlockSpec(memory_space=pltpu.SMEM)]
        + [pl.BlockSpec(memory_space=pl.ANY)] * len(blocks),
        out_specs=pl.BlockSpec(memory_space=pltpu.VMEM),
        scratch_shapes=[pltpu.SemaphoreType.DMA((strata,))],
        compiler_params=pltpu.CompilerParams(vmem_limit_bytes=VMEM_LIMIT),
        name="stage",
    )(meta, *blocks)


def code_row(staged_ref, stratum, blocks):
    code = staged_ref[stratum, blocks * LIVE :, :].astype(F32)
    return jnp.concatenate([code[b : b + 1] for b in range(blocks)], axis=1)


def chunk_step(users_live, ratings, items_old):
    predicted = dot(users_live, items_old, 1, 1)
    residual = (ratings.astype(F32) - predicted).astype(BF16)
    item_grad = dot(residual, users_live, 0, 0)
    wide = items_old.astype(F32)
    items_new = wide + learn_rate * (item_grad - shrink_rate * wide)
    return residual, items_new.astype(BF16)


def finish_users(users_old, residuals, items_old, staged_ref, stratum):
    blocks = users_old.shape[0] // LANES
    select = one_hot_rows(code_row(staged_ref, stratum, blocks), LIVE)
    residual = jnp.concatenate([r[...] for r in residuals], axis=1)
    spread = dot(select, residual, 0, 0).astype(BF16)
    grad = None
    step = spread.shape[1] // len(items_old)
    for k, chunk in enumerate(items_old):
        part = dot(spread[:, k * step : (k + 1) * step], chunk[...], 1, 0)
        grad = part if grad is None else grad + part
    wide = users_old.astype(F32)
    return (wide + learn_rate * (grad - shrink_rate * wide)).astype(BF16)


def ratings_of(staged_ref, stratum, chunk, per):
    first = chunk * per
    parts = [staged_ref[stratum, b * LIVE : (b + 1) * LIVE, :] for b in range(first, first + per)]
    return jnp.concatenate(parts, axis=1)


def live_rows(users, staged_ref, stratum):
    select = one_hot_rows(code_row(staged_ref, stratum, users.shape[0] // LANES), LIVE)
    return dot(select, users, 1, 0).astype(BF16)


def begin_kernel(staged_ref, users_ref, live_ref):
    live_ref[...] = live_rows(users_ref[...], staged_ref, 0)


def users_kernel(stratum, chunks, staged_ref, users_ref, *refs):
    residuals, items_before = refs[:chunks], refs[chunks : 2 * chunks]
    live_ref, users_out = refs[2 * chunks :]
    users = finish_users(users_ref[...], residuals, items_before, staged_ref, stratum)
    users_out[...] = users
    live_ref[...] = live_rows(users, staged_ref, stratum + 1)


def next_kernel(stratum, chunk, per, staged_ref, live_ref, items_ref, residual_ref, out_ref):
    ratings = ratings_of(staged_ref, stratum, chunk, per)
    residual, items_new = chunk_step(live_ref[...], ratings, items_ref[...])
    residual_ref[...] = residual
    out_ref[...] = items_new


def last_kernel(stratum, chunks, staged_ref, users_ref, *refs):
    residuals = refs[:chunks]
    items_before = refs[chunks : 2 * chunks]
    refs[2 * chunks][...] = finish_users(
        users_ref[...], residuals, items_before, staged_ref, stratum
    )


def run(kernel, operands, outs, flops, name):
    moved = sum(x.size * x.dtype.itemsize for x in outs) * 2
    vmem = pl.BlockSpec(memory_space=pltpu.VMEM)
    return pl.pallas_call(
        kernel,
        out_shape=[pltpu.VMEM(x.shape, x.dtype) for x in outs],
        in_specs=[vmem] * len(operands),
        out_specs=[vmem] * len(outs),
        cost_estimate=pl.CostEstimate(flops=flops, bytes_accessed=moved, transcendentals=0),
        compiler_params=pltpu.CompilerParams(vmem_limit_bytes=VMEM_LIMIT),
        name=name,
    )(*[pltpu.with_memory_space_constraint(x, pltpu.VMEM) for x in operands])


def passed_along(array, axis, by):
    peers = lax.axis_size(axis)
    return lax.ppermute(array, axis, [(i, (i + by) % peers) for i in range(peers)])


def local(logs, tile_rows, slot_owner, counts, owner_source, user_factors, item_factors):
    slots = logs.shape[0]
    strata = owner_source.shape[2]
    me = lax.axis_index("users").astype(jnp.int32)
    meta_out = jnp.concatenate([slot_owner[:, 0], counts[0], me[None]])
    meta_in = jnp.concatenate([owner_source[0, 0], me[None]])

    arrived, shifts = [], []
    for group in GROUPS:
        packed = compact(logs, tile_rows, meta_out, group, slots)
        for shift, block in zip(group, packed):
            shifts.append(shift)
            arrived.append(passed_along(block, "users", shift) if shift else block)
    staged = stage(arrived, tuple(shifts), meta_in, slots, strata)

    users = user_factors[0, 0]
    rows, rank = users.shape
    size = rows // CHUNKS
    per = size // LANES
    items = [item_factors[0, 0, k * size : (k + 1) * size] for k in range(CHUNKS)]
    live_shape = jax.ShapeDtypeStruct((LIVE, rank), BF16)
    residual_shape = jax.ShapeDtypeStruct((LIVE, size), BF16)
    chunk_shape = jax.ShapeDtypeStruct((size, rank), BF16)
    users_shape = jax.ShapeDtypeStruct((rows, rank), BF16)
    chunk_flops = 4 * LIVE * size * rank
    users_flops = 2 * rows * rows * (LIVE + rank)

    (live,) = run(begin_kernel, [staged, users], [live_shape], 2 * LIVE * rows * rank, "begin")
    for stratum in range(strata):
        residuals, outgoing, before = [], [], items
        by = 1 if stratum + 1 < strata else 1 - strata
        for k in range(CHUNKS):
            residual, moved = run(
                functools.partial(next_kernel, stratum, k, per),
                [staged, live, items[k]],
                [residual_shape, chunk_shape],
                chunk_flops,
                "next",
            )
            residuals.append(residual)
            outgoing.append(passed_along(moved, "items", by))
        items = outgoing
        if stratum + 1 < strata:
            live, users = run(
                functools.partial(users_kernel, stratum, CHUNKS),
                [staged, users] + residuals + before,
                [live_shape, users_shape],
                users_flops,
                "users",
            )
    (users,) = run(
        functools.partial(last_kernel, strata - 1, CHUNKS),
        [staged, users] + residuals + before,
        [users_shape],
        users_flops,
        "last",
    )
    return (users[None, None], jnp.concatenate(items, axis=0)[None, None])


def solution(mesh):
    placed = (
        P("users", "items", None, None),
        P("users", "items", None),
        P("users", "items"),
        P("users", "items"),
        P("users", "items", None),
        P("users", "items", None, None),
        P("users", "items", None, None),
    )
    return jax.shard_map(
        local,
        mesh=mesh,
        in_specs=placed,
        out_specs=(P("users", "items", None, None), P("users", "items", None, None)),
        check_vma=False,
    )
```

```python
import functools

import jax
import jax.numpy as jnp
from jax import lax
from jax.experimental import pallas as pl
from jax.experimental.pallas import tpu as pltpu
from jax.sharding import PartitionSpec as P


learn_rate = 0.01
shrink_rate = 0.05

LANES = 128
LIVE = 256
VMEM_LIMIT = 16 * 1024 * 1024
CHUNKS = 4
GROUPS = ((3,), (13, 15), (11, 7), (5, 9), (4, 8), (12, 2), (10, 6, 14, 1, 0))

F32 = jnp.float32
BF16 = jnp.bfloat16


def slot_for(owner, slot_owner, count, slots):
    found = jnp.int32(0)
    for slot in range(slots - 1, -1, -1):
        hit = (slot_owner[slot] == owner) & (slot < count)
        found = jnp.where(hit, jnp.int32(slot), found)
    return found


def dot(a, b, ca, cb):
    return lax.dot_general(a, b, (((ca,), (cb,)), ((), ())), preferred_element_type=F32)


def one_hot_rows(code, rows):
    lane_code = jnp.broadcast_to(code, (rows, code.shape[1]))
    row = lax.broadcasted_iota(jnp.int32, lane_code.shape, 0).astype(F32)
    return jnp.where(lane_code == row, 1.0, 0.0).astype(BF16)


def compact_kernel(group, slots, meta_ref, *refs):
    tiles = refs[: len(group)]
    marks_ref = refs[len(group)]
    outs = refs[-len(group) :]
    width = marks_ref.shape[2]
    blocks = width // LANES
    below = lax.broadcasted_iota(jnp.int32, (width, width), 0)
    upto = lax.broadcasted_iota(jnp.int32, (width, width), 1)
    ramp = jnp.where(below <= upto, 1.0, 0.0).astype(BF16)
    me = meta_ref[slots + 1]
    for place, shift in enumerate(group):
        slot = slot_for(lax.rem(me + shift, slots), meta_ref, meta_ref[slots], slots)
        marks = marks_ref[slot].astype(F32)
        marks8 = jnp.broadcast_to(marks, (8, width))
        order = dot(marks8.astype(BF16), ramp, 1, 0)
        code8 = jnp.where(marks8 > 0.5, order - 1.0, -1.0)
        select = one_hot_rows(code8[0:1], LIVE)
        packed = dot(select, tiles[place][0, 0], 1, 0).astype(BF16)
        sub = lax.broadcasted_iota(jnp.int32, (8, LANES), 0)
        tail = jnp.zeros((8, LANES), F32)
        for b in range(blocks):
            lanes = slice(b * LANES, (b + 1) * LANES)
            outs[place][b * LIVE : (b + 1) * LIVE, :] = packed[:, lanes]
            tail = jnp.where(sub == b, code8[:, lanes], tail)
        outs[place][blocks * LIVE :, :] = tail.astype(BF16)


def compact(logs, row_marks, meta, group, slots, after):
    width = logs.shape[2]
    rows = (width // LANES) * LIVE + 8

    def tile_map(shift):
        def index(step, meta_ref):
            owner = lax.rem(meta_ref[slots + 1] + shift, slots)
            return (slot_for(owner, meta_ref, meta_ref[slots], slots), 0, 0, 0)

        return index

    return pl.pallas_call(
        lambda *refs: compact_kernel(group, slots, *refs),
        out_shape=[jax.ShapeDtypeStruct((rows, LANES), BF16) for _ in group],
        grid_spec=pltpu.PrefetchScalarGridSpec(
            num_scalar_prefetch=1,
            grid=(1,),
            in_specs=[pl.BlockSpec((1, 1, width, width), tile_map(shift)) for shift in group]
            + [pl.BlockSpec(row_marks.shape, lambda step, meta_ref: (0, 0, 0))]
            + [pl.BlockSpec(memory_space=pl.ANY)] * len(after),
            out_specs=[pl.BlockSpec((rows, LANES), lambda step, meta_ref: (0, 0)) for _ in group],
        ),
        cost_estimate=pl.CostEstimate(
            flops=len(group) * 2 * LIVE * width * width,
            bytes_accessed=len(group) * 3 * width * width,
            transcendentals=0,
        ),
        compiler_params=pltpu.CompilerParams(vmem_limit_bytes=VMEM_LIMIT),
        name="compact",
    )(meta, *([logs] * len(group)), row_marks, *after)


def stage_kernel(shifts, slots, strata, meta_ref, *refs):
    blocks = refs[: len(shifts)]
    out_ref = refs[len(shifts)]
    sem = refs[len(shifts) + 1]
    me = meta_ref[strata]
    for s in range(strata):
        shift = lax.rem(me - meta_ref[s] + slots, slots)
        for place, d in enumerate(shifts):

            @pl.when(shift == d)
            def _():
                pltpu.make_async_copy(blocks[place], out_ref.at[s], sem.at[s]).start()

    for s in range(strata):
        pltpu.make_async_copy(blocks[0], out_ref.at[s], sem.at[s]).wait()


def stage(blocks, shifts, meta, slots, strata):
    rows, lanes = blocks[0].shape
    return pl.pallas_call(
        lambda *refs: stage_kernel(shifts, slots, strata, *refs),
        out_shape=pltpu.VMEM((strata, rows, lanes), BF16),
        in_specs=[pl.BlockSpec(memory_space=pltpu.SMEM)]
        + [pl.BlockSpec(memory_space=pl.ANY)] * len(blocks),
        out_specs=pl.BlockSpec(memory_space=pltpu.VMEM),
        scratch_shapes=[pltpu.SemaphoreType.DMA((strata,))],
        compiler_params=pltpu.CompilerParams(vmem_limit_bytes=VMEM_LIMIT),
        name="stage",
    )(meta, *blocks)


def code_row(staged_ref, stratum, blocks):
    code = staged_ref[stratum, blocks * LIVE :, :].astype(F32)
    return jnp.concatenate([code[b : b + 1] for b in range(blocks)], axis=1)


def chunk_step(users_live, ratings, items_old):
    predicted = dot(users_live, items_old, 1, 1)
    residual = (ratings.astype(F32) - predicted).astype(BF16)
    item_grad = dot(residual, users_live, 0, 0)
    wide = items_old.astype(F32)
    items_new = wide + learn_rate * (item_grad - shrink_rate * wide)
    return residual, items_new.astype(BF16)


def finish_users(users_old, residuals, items_old, staged_ref, stratum):
    blocks = users_old.shape[0] // LANES
    select = one_hot_rows(code_row(staged_ref, stratum, blocks), LIVE)
    residual = jnp.concatenate([r[...] for r in residuals], axis=1)
    spread = dot(select, residual, 0, 0).astype(BF16)
    grad = None
    step = spread.shape[1] // len(items_old)
    for k, chunk in enumerate(items_old):
        part = dot(spread[:, k * step : (k + 1) * step], chunk[...], 1, 0)
        grad = part if grad is None else grad + part
    wide = users_old.astype(F32)
    return (wide + learn_rate * (grad - shrink_rate * wide)).astype(BF16)


def ratings_of(staged_ref, stratum, chunk, per):
    first = chunk * per
    parts = [staged_ref[stratum, b * LIVE : (b + 1) * LIVE, :] for b in range(first, first + per)]
    return jnp.concatenate(parts, axis=1)


def live_rows(users, staged_ref, stratum):
    select = one_hot_rows(code_row(staged_ref, stratum, users.shape[0] // LANES), LIVE)
    return dot(select, users, 1, 0).astype(BF16)


def begin_kernel(staged_ref, users_ref, live_ref):
    live_ref[...] = live_rows(users_ref[...], staged_ref, 0)


def users_kernel(stratum, chunks, staged_ref, users_ref, *refs):
    residuals, items_before = refs[:chunks], refs[chunks : 2 * chunks]
    live_ref, users_out = refs[2 * chunks :]
    users = finish_users(users_ref[...], residuals, items_before, staged_ref, stratum)
    users_out[...] = users
    live_ref[...] = live_rows(users, staged_ref, stratum + 1)


def next_kernel(stratum, chunk, per, staged_ref, live_ref, items_ref, residual_ref, out_ref):
    ratings = ratings_of(staged_ref, stratum, chunk, per)
    residual, items_new = chunk_step(live_ref[...], ratings, items_ref[...])
    residual_ref[...] = residual
    out_ref[...] = items_new


def last_kernel(stratum, chunks, staged_ref, users_ref, *refs):
    residuals = refs[:chunks]
    items_before = refs[chunks : 2 * chunks]
    refs[2 * chunks][...] = finish_users(
        users_ref[...], residuals, items_before, staged_ref, stratum
    )


def run(kernel, operands, outs, flops, name):
    moved = sum(x.size * x.dtype.itemsize for x in outs) * 2
    vmem = pl.BlockSpec(memory_space=pltpu.VMEM)
    return pl.pallas_call(
        kernel,
        out_shape=[pltpu.VMEM(x.shape, x.dtype) for x in outs],
        in_specs=[vmem] * len(operands),
        out_specs=[vmem] * len(outs),
        cost_estimate=pl.CostEstimate(flops=flops, bytes_accessed=moved, transcendentals=0),
        compiler_params=pltpu.CompilerParams(vmem_limit_bytes=VMEM_LIMIT),
        name=name,
    )(*[pltpu.with_memory_space_constraint(x, pltpu.VMEM) for x in operands])


def passed_along(array, axis, by):
    peers = lax.axis_size(axis)
    return lax.ppermute(array, axis, [(i, (i + by) % peers) for i in range(peers)])


def local(logs, tile_rows, slot_owner, counts, owner_source, user_factors, item_factors):
    slots = logs.shape[0]
    strata = owner_source.shape[2]
    me = lax.axis_index("users").astype(jnp.int32)
    meta_out = jnp.concatenate([slot_owner[:, 0], counts[0], me[None]])
    meta_in = jnp.concatenate([owner_source[0, 0], me[None]])

    logs = pltpu.with_memory_space_constraint(logs, pltpu.HBM)
    marks = pltpu.with_memory_space_constraint(tile_rows, pltpu.HBM)
    arrived, shifts, packed = [], [], []
    for group in GROUPS:
        packed = compact(logs, marks, meta_out, group, slots, packed[:1])
        for shift, block in zip(group, packed):
            shifts.append(shift)
            arrived.append(passed_along(block, "users", shift) if shift else block)
    staged = stage(arrived, tuple(shifts), meta_in, slots, strata)

    users = user_factors[0, 0]
    rows, rank = users.shape
    size = rows // CHUNKS
    per = size // LANES
    items = [item_factors[0, 0, k * size : (k + 1) * size] for k in range(CHUNKS)]
    live_shape = jax.ShapeDtypeStruct((LIVE, rank), BF16)
    residual_shape = jax.ShapeDtypeStruct((LIVE, size), BF16)
    chunk_shape = jax.ShapeDtypeStruct((size, rank), BF16)
    users_shape = jax.ShapeDtypeStruct((rows, rank), BF16)
    chunk_flops = 4 * LIVE * size * rank
    users_flops = 2 * rows * rows * (LIVE + rank)

    (live,) = run(begin_kernel, [staged, users], [live_shape], 2 * LIVE * rows * rank, "begin")
    for stratum in range(strata):
        residuals, outgoing, before = [], [], items
        by = 1 if stratum + 1 < strata else 1 - strata
        for k in range(CHUNKS):
            residual, moved = run(
                functools.partial(next_kernel, stratum, k, per),
                [staged, live, items[k]],
                [residual_shape, chunk_shape],
                chunk_flops,
                "next",
            )
            residuals.append(residual)
            outgoing.append(passed_along(moved, "items", by))
        items = outgoing
        if stratum + 1 < strata:
            live, users = run(
                functools.partial(users_kernel, stratum, CHUNKS),
                [staged, users] + residuals + before,
                [live_shape, users_shape],
                users_flops,
                "users",
            )
    (users,) = run(
        functools.partial(last_kernel, strata - 1, CHUNKS),
        [staged, users] + residuals + before,
        [users_shape],
        users_flops,
        "last",
    )
    return (users[None, None], jnp.concatenate(items, axis=0)[None, None])


def solution(mesh):
    placed = (
        P("users", "items", None, None),
        P("users", "items", None),
        P("users", "items"),
        P("users", "items"),
        P("users", "items", None),
        P("users", "items", None, None),
        P("users", "items", None, None),
    )
    return jax.shard_map(
        local,
        mesh=mesh,
        in_specs=placed,
        out_specs=(P("users", "items", None, None), P("users", "items", None, None)),
        check_vma=False,
    )
```

```python
import functools

import jax
import jax.numpy as jnp
from jax import lax
from jax.experimental import pallas as pl
from jax.experimental.pallas import tpu as pltpu
from jax.sharding import PartitionSpec as P


learn_rate = 0.01
shrink_rate = 0.05

LANES = 128
LIVE = 256
VMEM_LIMIT = 16 * 1024 * 1024
CHUNKS = 4
GROUPS = ((4,), (12, 15), (3, 7), (13, 9), (11, 8), (5, 2), (10, 6, 14, 1, 0))

F32 = jnp.float32
BF16 = jnp.bfloat16


def slot_for(owner, slot_owner, count, slots):
    found = jnp.int32(0)
    for slot in range(slots - 1, -1, -1):
        hit = (slot_owner[slot] == owner) & (slot < count)
        found = jnp.where(hit, jnp.int32(slot), found)
    return found


def dot(a, b, ca, cb):
    return lax.dot_general(a, b, (((ca,), (cb,)), ((), ())), preferred_element_type=F32)


def one_hot_rows(code, rows):
    lane_code = jnp.broadcast_to(code, (rows, code.shape[1]))
    row = lax.broadcasted_iota(jnp.int32, lane_code.shape, 0).astype(F32)
    return jnp.where(lane_code == row, 1.0, 0.0).astype(BF16)


def compact_kernel(group, slots, meta_ref, *refs):
    tiles = refs[: len(group)]
    marks_ref = refs[len(group)]
    outs = refs[-len(group) :]
    width = marks_ref.shape[2]
    blocks = width // LANES
    below = lax.broadcasted_iota(jnp.int32, (width, width), 0)
    upto = lax.broadcasted_iota(jnp.int32, (width, width), 1)
    ramp = jnp.where(below <= upto, 1.0, 0.0).astype(BF16)
    me = meta_ref[slots + 1]
    for place, shift in enumerate(group):
        slot = slot_for(lax.rem(me + shift, slots), meta_ref, meta_ref[slots], slots)
        marks = marks_ref[slot].astype(F32)
        marks8 = jnp.broadcast_to(marks, (8, width))
        order = dot(marks8.astype(BF16), ramp, 1, 0)
        code8 = jnp.where(marks8 > 0.5, order - 1.0, -1.0)
        select = one_hot_rows(code8[0:1], LIVE)
        packed = dot(select, tiles[place][0, 0], 1, 0).astype(BF16)
        sub = lax.broadcasted_iota(jnp.int32, (8, LANES), 0)
        tail = jnp.zeros((8, LANES), F32)
        for b in range(blocks):
            lanes = slice(b * LANES, (b + 1) * LANES)
            outs[place][b * LIVE : (b + 1) * LIVE, :] = packed[:, lanes]
            tail = jnp.where(sub == b, code8[:, lanes], tail)
        outs[place][blocks * LIVE :, :] = tail.astype(BF16)


def compact(logs, row_marks, meta, group, slots, after):
    width = logs.shape[2]
    rows = (width // LANES) * LIVE + 8

    def tile_map(shift):
        def index(step, meta_ref):
            owner = lax.rem(meta_ref[slots + 1] + shift, slots)
            return (slot_for(owner, meta_ref, meta_ref[slots], slots), 0, 0, 0)

        return index

    return pl.pallas_call(
        lambda *refs: compact_kernel(group, slots, *refs),
        out_shape=[jax.ShapeDtypeStruct((rows, LANES), BF16) for _ in group],
        grid_spec=pltpu.PrefetchScalarGridSpec(
            num_scalar_prefetch=1,
            grid=(1,),
            in_specs=[pl.BlockSpec((1, 1, width, width), tile_map(shift)) for shift in group]
            + [pl.BlockSpec(row_marks.shape, lambda step, meta_ref: (0, 0, 0))]
            + [pl.BlockSpec(memory_space=pl.ANY)] * len(after),
            out_specs=[pl.BlockSpec((rows, LANES), lambda step, meta_ref: (0, 0)) for _ in group],
        ),
        cost_estimate=pl.CostEstimate(
            flops=len(group) * 2 * LIVE * width * width,
            bytes_accessed=len(group) * 3 * width * width,
            transcendentals=0,
        ),
        compiler_params=pltpu.CompilerParams(vmem_limit_bytes=VMEM_LIMIT),
        name="compact",
    )(meta, *([logs] * len(group)), row_marks, *after)


def stage_kernel(shifts, slots, strata, meta_ref, *refs):
    blocks = refs[: len(shifts)]
    out_ref = refs[len(shifts)]
    sem = refs[len(shifts) + 1]
    me = meta_ref[strata]
    for s in range(strata):
        shift = lax.rem(me - meta_ref[s] + slots, slots)
        for place, d in enumerate(shifts):

            @pl.when(shift == d)
            def _():
                pltpu.make_async_copy(blocks[place], out_ref.at[s], sem.at[s]).start()

    for s in range(strata):
        pltpu.make_async_copy(blocks[0], out_ref.at[s], sem.at[s]).wait()


def stage(blocks, shifts, meta, slots, strata):
    rows, lanes = blocks[0].shape
    return pl.pallas_call(
        lambda *refs: stage_kernel(shifts, slots, strata, *refs),
        out_shape=pltpu.VMEM((strata, rows, lanes), BF16),
        in_specs=[pl.BlockSpec(memory_space=pltpu.SMEM)]
        + [pl.BlockSpec(memory_space=pl.ANY)] * len(blocks),
        out_specs=pl.BlockSpec(memory_space=pltpu.VMEM),
        scratch_shapes=[pltpu.SemaphoreType.DMA((strata,))],
        compiler_params=pltpu.CompilerParams(vmem_limit_bytes=VMEM_LIMIT),
        name="stage",
    )(meta, *blocks)


def code_row(staged_ref, stratum, blocks):
    code = staged_ref[stratum, blocks * LIVE :, :].astype(F32)
    return jnp.concatenate([code[b : b + 1] for b in range(blocks)], axis=1)


def chunk_step(users_live, ratings, items_old):
    predicted = dot(users_live, items_old, 1, 1)
    residual = (ratings.astype(F32) - predicted).astype(BF16)
    item_grad = dot(residual, users_live, 0, 0)
    wide = items_old.astype(F32)
    items_new = wide + learn_rate * (item_grad - shrink_rate * wide)
    return residual, items_new.astype(BF16)


def finish_users(users_old, residuals, items_old, staged_ref, stratum):
    blocks = users_old.shape[0] // LANES
    select = one_hot_rows(code_row(staged_ref, stratum, blocks), LIVE)
    residual = jnp.concatenate([r[...] for r in residuals], axis=1)
    spread = dot(select, residual, 0, 0).astype(BF16)
    grad = None
    step = spread.shape[1] // len(items_old)
    for k, chunk in enumerate(items_old):
        part = dot(spread[:, k * step : (k + 1) * step], chunk[...], 1, 0)
        grad = part if grad is None else grad + part
    wide = users_old.astype(F32)
    return (wide + learn_rate * (grad - shrink_rate * wide)).astype(BF16)


def ratings_of(staged_ref, stratum, chunk, per):
    first = chunk * per
    parts = [staged_ref[stratum, b * LIVE : (b + 1) * LIVE, :] for b in range(first, first + per)]
    return jnp.concatenate(parts, axis=1)


def live_rows(users, staged_ref, stratum):
    select = one_hot_rows(code_row(staged_ref, stratum, users.shape[0] // LANES), LIVE)
    return dot(select, users, 1, 0).astype(BF16)


def begin_kernel(staged_ref, users_ref, live_ref):
    live_ref[...] = live_rows(users_ref[...], staged_ref, 0)


def users_kernel(stratum, chunks, staged_ref, users_ref, *refs):
    residuals, items_before = refs[:chunks], refs[chunks : 2 * chunks]
    live_ref, users_out = refs[2 * chunks :]
    users = finish_users(users_ref[...], residuals, items_before, staged_ref, stratum)
    users_out[...] = users
    live_ref[...] = live_rows(users, staged_ref, stratum + 1)


def next_kernel(stratum, chunk, per, staged_ref, live_ref, items_ref, residual_ref, out_ref):
    ratings = ratings_of(staged_ref, stratum, chunk, per)
    residual, items_new = chunk_step(live_ref[...], ratings, items_ref[...])
    residual_ref[...] = residual
    out_ref[...] = items_new


def last_kernel(stratum, chunks, staged_ref, users_ref, *refs):
    residuals = refs[:chunks]
    items_before = refs[chunks : 2 * chunks]
    refs[2 * chunks][...] = finish_users(
        users_ref[...], residuals, items_before, staged_ref, stratum
    )


def run(kernel, operands, outs, flops, name):
    moved = sum(x.size * x.dtype.itemsize for x in outs) * 2
    vmem = pl.BlockSpec(memory_space=pltpu.VMEM)
    return pl.pallas_call(
        kernel,
        out_shape=[pltpu.VMEM(x.shape, x.dtype) for x in outs],
        in_specs=[vmem] * len(operands),
        out_specs=[vmem] * len(outs),
        cost_estimate=pl.CostEstimate(flops=flops, bytes_accessed=moved, transcendentals=0),
        compiler_params=pltpu.CompilerParams(vmem_limit_bytes=VMEM_LIMIT),
        name=name,
    )(*[pltpu.with_memory_space_constraint(x, pltpu.VMEM) for x in operands])


def passed_along(array, axis, by):
    peers = lax.axis_size(axis)
    return lax.ppermute(array, axis, [(i, (i + by) % peers) for i in range(peers)])


def local(logs, tile_rows, slot_owner, counts, owner_source, user_factors, item_factors):
    slots = logs.shape[0]
    strata = owner_source.shape[2]
    me = lax.axis_index("users").astype(jnp.int32)
    meta_out = jnp.concatenate([slot_owner[:, 0], counts[0], me[None]])
    meta_in = jnp.concatenate([owner_source[0, 0], me[None]])

    logs = pltpu.with_memory_space_constraint(logs, pltpu.HBM)
    marks = pltpu.with_memory_space_constraint(tile_rows, pltpu.HBM)
    arrived, shifts, packed = [], [], []
    for group in GROUPS:
        packed = compact(logs, marks, meta_out, group, slots, packed[:1])
        for shift, block in zip(group, packed):
            shifts.append(shift)
            arrived.append(passed_along(block, "users", shift) if shift else block)
    staged = stage(arrived, tuple(shifts), meta_in, slots, strata)

    users = user_factors[0, 0]
    rows, rank = users.shape
    size = rows // CHUNKS
    per = size // LANES
    items = [item_factors[0, 0, k * size : (k + 1) * size] for k in range(CHUNKS)]
    live_shape = jax.ShapeDtypeStruct((LIVE, rank), BF16)
    residual_shape = jax.ShapeDtypeStruct((LIVE, size), BF16)
    chunk_shape = jax.ShapeDtypeStruct((size, rank), BF16)
    users_shape = jax.ShapeDtypeStruct((rows, rank), BF16)
    chunk_flops = 4 * LIVE * size * rank
    users_flops = 2 * rows * rows * (LIVE + rank)

    (live,) = run(begin_kernel, [staged, users], [live_shape], 2 * LIVE * rows * rank, "begin")
    for stratum in range(strata):
        residuals, outgoing, before = [], [], items
        by = 1 if stratum + 1 < strata else 1 - strata
        for k in range(CHUNKS):
            residual, moved = run(
                functools.partial(next_kernel, stratum, k, per),
                [staged, live, items[k]],
                [residual_shape, chunk_shape],
                chunk_flops,
                "next",
            )
            residuals.append(residual)
            outgoing.append(passed_along(moved, "items", by))
        items = outgoing
        if stratum + 1 < strata:
            live, users = run(
                functools.partial(users_kernel, stratum, CHUNKS),
                [staged, users] + residuals + before,
                [live_shape, users_shape],
                users_flops,
                "users",
            )
    (users,) = run(
        functools.partial(last_kernel, strata - 1, CHUNKS),
        [staged, users] + residuals + before,
        [users_shape],
        users_flops,
        "last",
    )
    return (users[None, None], jnp.concatenate(items, axis=0)[None, None])


def solution(mesh):
    placed = (
        P("users", "items", None, None),
        P("users", "items", None),
        P("users", "items"),
        P("users", "items"),
        P("users", "items", None),
        P("users", "items", None, None),
        P("users", "items", None, None),
    )
    return jax.shard_map(
        local,
        mesh=mesh,
        in_specs=placed,
        out_specs=(P("users", "items", None, None), P("users", "items", None, None)),
        check_vma=False,
    )
```

```python
import functools

import jax
import jax.numpy as jnp
from jax import lax
from jax.experimental import pallas as pl
from jax.experimental.pallas import tpu as pltpu
from jax.sharding import PartitionSpec as P


learn_rate = 0.01
shrink_rate = 0.05

LANES = 128
LIVE = 256
VMEM_LIMIT = 16 * 1024 * 1024
CHUNKS = 2
EVEN, ODD = 0, 1
GROUPS = ((4,), (12, 15), (3, 7), (13, 9), (11, 8), (5, 2), (10, 6, 14, 1, 0))

F32 = jnp.float32
BF16 = jnp.bfloat16


def slot_for(owner, slot_owner, count, slots):
    found = jnp.int32(0)
    for slot in range(slots - 1, -1, -1):
        hit = (slot_owner[slot] == owner) & (slot < count)
        found = jnp.where(hit, jnp.int32(slot), found)
    return found


def dot(a, b, ca, cb):
    return lax.dot_general(a, b, (((ca,), (cb,)), ((), ())), preferred_element_type=F32)


def one_hot_rows(code, rows):
    lane_code = jnp.broadcast_to(code, (rows, code.shape[1]))
    row = lax.broadcasted_iota(jnp.int32, lane_code.shape, 0).astype(F32)
    return jnp.where(lane_code == row, 1.0, 0.0).astype(BF16)


def compact_kernel(group, slots, meta_ref, *refs):
    tiles = refs[: len(group)]
    marks_ref = refs[len(group)]
    outs = refs[-len(group) :]
    width = marks_ref.shape[2]
    blocks = width // LANES
    below = lax.broadcasted_iota(jnp.int32, (width, width), 0)
    upto = lax.broadcasted_iota(jnp.int32, (width, width), 1)
    ramp = jnp.where(below <= upto, 1.0, 0.0).astype(BF16)
    me = meta_ref[slots + 1]
    for place, shift in enumerate(group):
        slot = slot_for(lax.rem(me + shift, slots), meta_ref, meta_ref[slots], slots)
        marks = marks_ref[slot].astype(F32)
        marks8 = jnp.broadcast_to(marks, (8, width))
        order = dot(marks8.astype(BF16), ramp, 1, 0)
        code8 = jnp.where(marks8 > 0.5, order - 1.0, -1.0)
        select = one_hot_rows(code8[0:1], LIVE)
        packed = dot(select, tiles[place][0, 0], 1, 0).astype(BF16)
        sub = lax.broadcasted_iota(jnp.int32, (8, LANES), 0)
        tail = jnp.zeros((8, LANES), F32)
        for b in range(blocks):
            lanes = slice(b * LANES, (b + 1) * LANES)
            outs[place][b * LIVE : (b + 1) * LIVE, :] = packed[:, lanes]
            tail = jnp.where(sub == b, code8[:, lanes], tail)
        outs[place][blocks * LIVE :, :] = tail.astype(BF16)


def compact(logs, row_marks, meta, group, slots, after):
    width = logs.shape[2]
    rows = (width // LANES) * LIVE + 8

    def tile_map(shift):
        def index(step, meta_ref):
            owner = lax.rem(meta_ref[slots + 1] + shift, slots)
            return (slot_for(owner, meta_ref, meta_ref[slots], slots), 0, 0, 0)

        return index

    return pl.pallas_call(
        lambda *refs: compact_kernel(group, slots, *refs),
        out_shape=[jax.ShapeDtypeStruct((rows, LANES), BF16) for _ in group],
        grid_spec=pltpu.PrefetchScalarGridSpec(
            num_scalar_prefetch=1,
            grid=(1,),
            in_specs=[pl.BlockSpec((1, 1, width, width), tile_map(shift)) for shift in group]
            + [pl.BlockSpec(row_marks.shape, lambda step, meta_ref: (0, 0, 0))]
            + [pl.BlockSpec(memory_space=pl.ANY)] * len(after),
            out_specs=[pl.BlockSpec((rows, LANES), lambda step, meta_ref: (0, 0)) for _ in group],
        ),
        cost_estimate=pl.CostEstimate(
            flops=len(group) * 2 * LIVE * width * width,
            bytes_accessed=len(group) * 3 * width * width,
            transcendentals=0,
        ),
        compiler_params=pltpu.CompilerParams(vmem_limit_bytes=VMEM_LIMIT),
        name="compact",
    )(meta, *([logs] * len(group)), row_marks, *after)


def stage_kernel(shifts, slots, strata, meta_ref, *refs):
    blocks = refs[: len(shifts)]
    out_ref = refs[len(shifts)]
    sem = refs[len(shifts) + 1]
    me = meta_ref[strata]
    for s in range(strata):
        shift = lax.rem(me - meta_ref[s] + slots, slots)
        for place, d in enumerate(shifts):

            @pl.when(shift == d)
            def _():
                pltpu.make_async_copy(blocks[place], out_ref.at[s], sem.at[s]).start()

    for s in range(strata):
        pltpu.make_async_copy(blocks[0], out_ref.at[s], sem.at[s]).wait()


def stage(blocks, shifts, meta, slots, strata):
    rows, lanes = blocks[0].shape
    return pl.pallas_call(
        lambda *refs: stage_kernel(shifts, slots, strata, *refs),
        out_shape=pltpu.VMEM((strata, rows, lanes), BF16),
        in_specs=[pl.BlockSpec(memory_space=pltpu.SMEM)]
        + [pl.BlockSpec(memory_space=pl.ANY)] * len(blocks),
        out_specs=pl.BlockSpec(memory_space=pltpu.VMEM),
        scratch_shapes=[pltpu.SemaphoreType.DMA((strata,))],
        compiler_params=pltpu.CompilerParams(vmem_limit_bytes=VMEM_LIMIT),
        name="stage",
    )(meta, *blocks)


def code_tail(staged_ref, stratum):
    rows = staged_ref.shape[1]
    return staged_ref[stratum, rows - 8 :, :].astype(F32)


def fill_live(staged_ref, stratum, users_ref, live_ref):
    tail = code_tail(staged_ref, stratum)
    blocks = users_ref.shape[0] // LANES
    code = jnp.concatenate([tail[b : b + 1] for b in range(blocks)], axis=1)
    code = jnp.broadcast_to(code, (LANES, code.shape[1]))
    row = lax.broadcasted_iota(jnp.int32, code.shape, 0)

    def band(step, carry):
        start = pl.multiple_of(step * LANES, LANES)
        select = jnp.where(code == (row + start).astype(F32), 1.0, 0.0).astype(BF16)
        live_ref[pl.ds(start, LANES), :] = dot(select, users_ref[...], 1, 0).astype(BF16)
        return carry

    lax.fori_loop(0, LIVE // LANES, band, 0)


def my_role():
    return lax.rem(lax.axis_index("items"), 2)


def begin_kernel(staged_ref, users_ref, live_ref):
    fill_live(staged_ref, 0, users_ref, live_ref)


def next_kernel(role, stratum, chunk, per, staged_ref, live_ref, items_ref, residual_ref, out_ref):
    @pl.when(my_role() == role)
    def _():
        def block(b, carry):
            rows = pl.ds(pl.multiple_of(b * LANES, LANES), LANES)
            kept = pl.ds(pl.multiple_of(b * LIVE, LIVE), LIVE)
            first = chunk * per * LIVE
            read = pl.ds(pl.multiple_of(first + b * LIVE, LIVE), LIVE)
            items_old = items_ref[rows, :]
            predicted = dot(live_ref[...], items_old, 1, 1)
            residual = (staged_ref[stratum, read, :].astype(F32) - predicted).astype(BF16)
            residual_ref[kept, :] = residual
            item_grad = dot(residual, live_ref[...], 0, 0)
            wide = items_old.astype(F32)
            items_new = wide + learn_rate * (item_grad - shrink_rate * wide)
            out_ref[rows, :] = items_new.astype(BF16)
            return carry

        lax.fori_loop(0, per, block, 0)


def users_kernel(role, stratum, last, chunks, staged_ref, users_ref, live_ref, *refs):
    residuals, items_before = refs[:chunks], refs[chunks : 2 * chunks]
    users_out, live_out = refs[2 * chunks :]
    size = items_before[0].shape[0]
    per = size // LANES

    @pl.when(my_role() == role)
    def _():
        tail = code_tail(staged_ref, stratum)
        sub = lax.broadcasted_iota(jnp.int32, tail.shape, 0)
        row = lax.broadcasted_iota(jnp.int32, (LIVE, LANES), 0).astype(F32)

        def block(b, carry):
            rows = pl.ds(pl.multiple_of(b * LANES, LANES), LANES)
            code = jnp.sum(jnp.where(sub == b, tail, 0.0), axis=0, keepdims=True)
            code = jnp.broadcast_to(code, row.shape)
            select = jnp.where(code == row, 1.0, 0.0).astype(BF16)
            grad = None
            for residual, chunk in zip(residuals, items_before):
                parts = [residual[c * LIVE : (c + 1) * LIVE, :] for c in range(per)]
                compacted = jnp.concatenate(parts, axis=1)
                spread = dot(select, compacted, 0, 0).astype(BF16)
                part = dot(spread, chunk[...], 1, 0)
                grad = part if grad is None else grad + part
            wide = users_ref[rows, :].astype(F32)
            new = wide + learn_rate * (grad - shrink_rate * wide)
            users_out[rows, :] = new.astype(BF16)
            return carry

        lax.fori_loop(0, users_ref.shape[0] // LANES, block, 0)
        if not last:
            fill_live(staged_ref, stratum + 1, users_out, live_out)


def run(kernel, operands, outs, flops, aliases={}):
    moved = sum(x.size * x.dtype.itemsize for x in outs) * 2
    vmem = pl.BlockSpec(memory_space=pltpu.VMEM)
    return pl.pallas_call(
        kernel,
        out_shape=[pltpu.VMEM(x.shape, x.dtype) for x in outs],
        in_specs=[vmem] * len(operands),
        out_specs=[vmem] * len(outs),
        cost_estimate=pl.CostEstimate(flops=flops, bytes_accessed=moved, transcendentals=0),
        compiler_params=pltpu.CompilerParams(vmem_limit_bytes=VMEM_LIMIT),
        input_output_aliases=aliases,
    )(*[pltpu.with_memory_space_constraint(x, pltpu.VMEM) for x in operands])


def passed_along(array, axis, by, role=None):
    peers = lax.axis_size(axis)
    sources = [i for i in range(peers) if role is None or i % 2 == role]
    return lax.ppermute(array, axis, [(i, (i + by) % peers) for i in sources])


def local(logs, tile_rows, slot_owner, counts, owner_source, user_factors, item_factors):
    slots = logs.shape[0]
    strata = owner_source.shape[2]
    me = lax.axis_index("users").astype(jnp.int32)
    meta_out = jnp.concatenate([slot_owner[:, 0], counts[0], me[None]])
    meta_in = jnp.concatenate([owner_source[0, 0], me[None]])

    logs = pltpu.with_memory_space_constraint(logs, pltpu.HBM)
    marks = pltpu.with_memory_space_constraint(tile_rows, pltpu.HBM)
    arrived, shifts, packed = [], [], []
    for group in GROUPS:
        packed = compact(logs, marks, meta_out, group, slots, packed[:1])
        for shift, block in zip(group, packed):
            shifts.append(shift)
            arrived.append(passed_along(block, "users", shift) if shift else block)
    staged = stage(arrived, tuple(shifts), meta_in, slots, strata)

    users = user_factors[0, 0]
    rows, rank = users.shape
    size = rows // CHUNKS
    per = size // LANES
    own = [item_factors[0, 0, k * size : (k + 1) * size] for k in range(CHUNKS)]
    live_shape = jax.ShapeDtypeStruct((LIVE, rank), BF16)
    residual_shape = jax.ShapeDtypeStruct((LIVE * per, LANES), BF16)
    chunk_shape = jax.ShapeDtypeStruct((size, rank), BF16)
    users_shape = jax.ShapeDtypeStruct((rows, rank), BF16)
    chunk_flops = 4 * LIVE * size * rank
    users_flops = 2 * rows * rows * (LIVE + rank)

    (live,) = run(begin_kernel, [staged, users], [live_shape], 2 * LIVE * rows * rank)
    held = {ODD: own, EVEN: own}
    for stratum in range(strata):
        last = stratum + 1 == strata
        sent = {}
        for role in (ODD, EVEN):
            residuals, sent[role] = [], []
            for k in range(CHUNKS):
                residual, moved = run(
                    functools.partial(next_kernel, role, stratum, k, per),
                    [staged, live, held[role][k]],
                    [residual_shape, chunk_shape],
                    chunk_flops,
                )
                residuals.append(residual)
                by = 1 - strata if last else 1
                sent[role].append(passed_along(moved, "items", by, role))
            users, live = run(
                functools.partial(users_kernel, role, stratum, last, CHUNKS),
                [staged, users, live] + residuals + held[role],
                [users_shape, live_shape],
                users_flops,
                {1: 0, 2: 1},
            )
        held = {ODD: sent[EVEN], EVEN: sent[ODD]}
    odd = lax.axis_index("items") % 2 == 1
    home = [jnp.where(odd, held[ODD][k], held[EVEN][k]) for k in range(CHUNKS)]
    return (users[None, None], jnp.concatenate(home, axis=0)[None, None])


def solution(mesh):
    placed = (
        P("users", "items", None, None),
        P("users", "items", None),
        P("users", "items"),
        P("users", "items"),
        P("users", "items", None),
        P("users", "items", None, None),
        P("users", "items", None, None),
    )
    return jax.shard_map(
        local,
        mesh=mesh,
        in_specs=placed,
        out_specs=(P("users", "items", None, None), P("users", "items", None, None)),
        check_vma=False,
    )
```

```python
import functools

import jax
import jax.numpy as jnp
from jax import lax
from jax.experimental import pallas as pl
from jax.experimental.pallas import tpu as pltpu
from jax.sharding import PartitionSpec as P


learn_rate = 0.01
shrink_rate = 0.05

LANES = 128
LIVE = 256
VMEM_LIMIT = 16 * 1024 * 1024
CHUNKS = 4
LAST_COUNT = 2
GROUPS = ((4,), (12, 15), (3, 7), (13, 9), (11, 8), (5, 2), (10, 6, 14, 1, 0))

F32 = jnp.float32
BF16 = jnp.bfloat16


def slot_for(owner, slot_owner, count, slots):
    found = jnp.int32(0)
    for slot in range(slots - 1, -1, -1):
        hit = (slot_owner[slot] == owner) & (slot < count)
        found = jnp.where(hit, jnp.int32(slot), found)
    return found


def dot(a, b, ca, cb):
    return lax.dot_general(a, b, (((ca,), (cb,)), ((), ())), preferred_element_type=F32)


def one_hot_rows(code, rows):
    lane_code = jnp.broadcast_to(code, (rows, code.shape[1]))
    row = lax.broadcasted_iota(jnp.int32, lane_code.shape, 0).astype(F32)
    return jnp.where(lane_code == row, 1.0, 0.0).astype(BF16)


def compact_kernel(group, slots, meta_ref, *refs):
    tiles = refs[: len(group)]
    marks_ref = refs[len(group)]
    outs = refs[-len(group) :]
    width = marks_ref.shape[2]
    blocks = width // LANES
    below = lax.broadcasted_iota(jnp.int32, (width, width), 0)
    upto = lax.broadcasted_iota(jnp.int32, (width, width), 1)
    ramp = jnp.where(below <= upto, 1.0, 0.0).astype(BF16)
    me = meta_ref[slots + 1]
    for place, shift in enumerate(group):
        slot = slot_for(lax.rem(me + shift, slots), meta_ref, meta_ref[slots], slots)
        marks = marks_ref[slot].astype(F32)
        marks8 = jnp.broadcast_to(marks, (8, width))
        order = dot(marks8.astype(BF16), ramp, 1, 0)
        code8 = jnp.where(marks8 > 0.5, order - 1.0, -1.0)
        select = one_hot_rows(code8[0:1], LIVE)
        packed = dot(select, tiles[place][0, 0], 1, 0).astype(BF16)
        sub = lax.broadcasted_iota(jnp.int32, (8, LANES), 0)
        tail = jnp.zeros((8, LANES), F32)
        for b in range(blocks):
            lanes = slice(b * LANES, (b + 1) * LANES)
            outs[place][b * LIVE : (b + 1) * LIVE, :] = packed[:, lanes]
            tail = jnp.where(sub == b, code8[:, lanes], tail)
        outs[place][blocks * LIVE :, :] = tail.astype(BF16)


def compact(logs, row_marks, meta, group, slots, after):
    width = logs.shape[2]
    rows = (width // LANES) * LIVE + 8

    def tile_map(shift):
        def index(step, meta_ref):
            owner = lax.rem(meta_ref[slots + 1] + shift, slots)
            return (slot_for(owner, meta_ref, meta_ref[slots], slots), 0, 0, 0)

        return index

    return pl.pallas_call(
        lambda *refs: compact_kernel(group, slots, *refs),
        out_shape=[jax.ShapeDtypeStruct((rows, LANES), BF16) for _ in group],
        grid_spec=pltpu.PrefetchScalarGridSpec(
            num_scalar_prefetch=1,
            grid=(1,),
            in_specs=[pl.BlockSpec((1, 1, width, width), tile_map(shift)) for shift in group]
            + [pl.BlockSpec(row_marks.shape, lambda step, meta_ref: (0, 0, 0))]
            + [pl.BlockSpec(memory_space=pl.ANY)] * len(after),
            out_specs=[pl.BlockSpec((rows, LANES), lambda step, meta_ref: (0, 0)) for _ in group],
        ),
        cost_estimate=pl.CostEstimate(
            flops=len(group) * 2 * LIVE * width * width,
            bytes_accessed=len(group) * 3 * width * width,
            transcendentals=0,
        ),
        compiler_params=pltpu.CompilerParams(vmem_limit_bytes=VMEM_LIMIT),
        name="compact",
    )(meta, *([logs] * len(group)), row_marks, *after)


def stage_kernel(shifts, slots, strata, meta_ref, *refs):
    blocks = refs[: len(shifts)]
    out_ref = refs[len(shifts)]
    sem = refs[len(shifts) + 1]
    me = meta_ref[strata]
    for s in range(strata):
        shift = lax.rem(me - meta_ref[s] + slots, slots)
        for place, d in enumerate(shifts):

            @pl.when(shift == d)
            def _():
                pltpu.make_async_copy(blocks[place], out_ref.at[s], sem.at[s]).start()

    for s in range(strata):
        pltpu.make_async_copy(blocks[0], out_ref.at[s], sem.at[s]).wait()


def stage(blocks, shifts, meta, slots, strata):
    rows, lanes = blocks[0].shape
    return pl.pallas_call(
        lambda *refs: stage_kernel(shifts, slots, strata, *refs),
        out_shape=pltpu.VMEM((strata, rows, lanes), BF16),
        in_specs=[pl.BlockSpec(memory_space=pltpu.SMEM)]
        + [pl.BlockSpec(memory_space=pl.ANY)] * len(blocks),
        out_specs=pl.BlockSpec(memory_space=pltpu.VMEM),
        scratch_shapes=[pltpu.SemaphoreType.DMA((strata,))],
        compiler_params=pltpu.CompilerParams(vmem_limit_bytes=VMEM_LIMIT),
        name="stage",
    )(meta, *blocks)


def code_tail(staged_ref, stratum):
    rows = staged_ref.shape[1]
    return staged_ref[stratum, rows - 8 :, :].astype(F32)


def fill_live(staged_ref, stratum, users_ref, live_ref):
    tail = code_tail(staged_ref, stratum)
    blocks = users_ref.shape[0] // LANES
    code = jnp.concatenate([tail[b : b + 1] for b in range(blocks)], axis=1)
    code = jnp.broadcast_to(code, (LANES, code.shape[1]))
    row = lax.broadcasted_iota(jnp.int32, code.shape, 0)

    def band(step, carry):
        start = pl.multiple_of(step * LANES, LANES)
        select = jnp.where(code == (row + start).astype(F32), 1.0, 0.0).astype(BF16)
        live_ref[pl.ds(start, LANES), :] = dot(select, users_ref[...], 1, 0).astype(BF16)
        return carry

    lax.fori_loop(0, LIVE // LANES, band, 0)


def begin_kernel(staged_ref, users_ref, live_ref):
    fill_live(staged_ref, 0, users_ref, live_ref)


def next_kernel(stratum, first, count, staged_ref, live_ref, *refs):
    items_refs, residual_refs, out_ref = refs[:count], refs[count : 2 * count], refs[2 * count]
    half = live_ref.shape[1] // 2
    for place in range(count):
        start = (first + place) * LIVE
        items_ref = items_refs[place]
        predicted = dot(live_ref[...], items_ref[...], 1, 1)
        ratings = staged_ref[stratum, start : start + LIVE, :].astype(F32)
        residual = (ratings - predicted).astype(BF16)
        residual_refs[place][...] = residual

        def side(step, carry):
            lanes = pl.ds(pl.multiple_of(step * half, half), half)
            item_grad = dot(residual_refs[place][...], live_ref[:, lanes], 0, 0)
            wide = items_ref[:, lanes].astype(F32)
            items_new = wide + learn_rate * (item_grad - shrink_rate * wide)
            out_ref[place * LANES : (place + 1) * LANES, lanes] = items_new.astype(BF16)
            return carry

        lax.fori_loop(0, 2, side, 0)


def users_kernel(stratum, last, chunks, staged_ref, users_ref, *refs):
    residuals, items_before = refs[:chunks], refs[chunks : 2 * chunks]
    users_out = refs[2 * chunks]
    tail = code_tail(staged_ref, stratum)
    sub = lax.broadcasted_iota(jnp.int32, tail.shape, 0)
    row = lax.broadcasted_iota(jnp.int32, (LIVE, LANES), 0).astype(F32)

    def block(b, carry):
        rows = pl.ds(pl.multiple_of(b * LANES, LANES), LANES)
        code = jnp.sum(jnp.where(sub == b, tail, 0.0), axis=0, keepdims=True)
        select = jnp.where(jnp.broadcast_to(code, row.shape) == row, 1.0, 0.0).astype(BF16)
        compacted = jnp.concatenate([residual[...] for residual in residuals], axis=1)
        spread = dot(select, compacted, 0, 0).astype(BF16)
        grad = None
        for k, chunk in enumerate(items_before):
            part = dot(spread[:, k * LANES : (k + 1) * LANES], chunk[...], 1, 0)
            grad = part if grad is None else grad + part
        wide = users_ref[rows, :].astype(F32)
        new = wide + learn_rate * (grad - shrink_rate * wide)
        users_out[rows, :] = new.astype(BF16)
        return carry

    lax.fori_loop(0, users_ref.shape[0] // LANES, block, 0)
    if not last:
        fill_live(staged_ref, stratum + 1, users_out, refs[2 * chunks + 1])


def run(kernel, operands, outs, flops, name, aliases={}):
    moved = sum(x.size * x.dtype.itemsize for x in outs) * 2
    vmem = pl.BlockSpec(memory_space=pltpu.VMEM)
    return pl.pallas_call(
        kernel,
        out_shape=[pltpu.VMEM(x.shape, x.dtype) for x in outs],
        in_specs=[vmem] * len(operands),
        out_specs=[vmem] * len(outs),
        cost_estimate=pl.CostEstimate(flops=flops, bytes_accessed=moved, transcendentals=0),
        compiler_params=pltpu.CompilerParams(vmem_limit_bytes=VMEM_LIMIT),
        input_output_aliases=aliases,
        name=name,
    )(*[pltpu.with_memory_space_constraint(x, pltpu.VMEM) for x in operands])


def passed_along(array, axis, by):
    peers = lax.axis_size(axis)
    return lax.ppermute(array, axis, [(i, (i + by) % peers) for i in range(peers)])


def local(logs, tile_rows, slot_owner, counts, owner_source, user_factors, item_factors):
    slots = logs.shape[0]
    strata = owner_source.shape[2]
    me = lax.axis_index("users").astype(jnp.int32)
    meta_out = jnp.concatenate([slot_owner[:, 0], counts[0], me[None]])
    meta_in = jnp.concatenate([owner_source[0, 0], me[None]])

    logs = pltpu.with_memory_space_constraint(logs, pltpu.HBM)
    marks = pltpu.with_memory_space_constraint(tile_rows, pltpu.HBM)
    arrived, shifts, packed = [], [], []
    for group in GROUPS:
        packed = compact(logs, marks, meta_out, group, slots, packed[:1])
        for shift, block in zip(group, packed):
            shifts.append(shift)
            arrived.append(passed_along(block, "users", shift) if shift else block)
    staged = stage(arrived, tuple(shifts), meta_in, slots, strata)

    users = user_factors[0, 0]
    rows, rank = users.shape
    size = rows // CHUNKS
    items = [item_factors[0, 0, k * size : (k + 1) * size] for k in range(CHUNKS)]
    live_shape = jax.ShapeDtypeStruct((LIVE, rank), BF16)
    residual_shape = jax.ShapeDtypeStruct((LIVE, size), BF16)
    users_shape = jax.ShapeDtypeStruct((rows, rank), BF16)
    chunk_flops = 4 * LIVE * size * rank
    users_flops = 2 * rows * rows * (LIVE + rank)

    (live,) = run(begin_kernel, [staged, users], [live_shape], 2 * LIVE * rows * rank, "begin")
    for stratum in range(strata):
        last = stratum + 1 == strata
        residuals, outgoing, before = [], [], items
        count = LAST_COUNT if last else 1
        by = 1 - strata if last else 1
        for k in range(0, CHUNKS, count):
            *parts, moved = run(
                functools.partial(next_kernel, stratum, k, count),
                [staged, live] + items[k : k + count],
                [residual_shape] * count + [jax.ShapeDtypeStruct((count * size, rank), BF16)],
                chunk_flops * count,
                "next",
            )
            residuals += parts
            outgoing.append(passed_along(moved, "items", by))
        items = outgoing
        users, *rest = run(
            functools.partial(users_kernel, stratum, last, CHUNKS),
            [staged, users] + residuals + before,
            [users_shape] if last else [users_shape, live_shape],
            users_flops,
            "users",
        )
        live = None if last else rest[0]
    return (users[None, None], jnp.concatenate(items, axis=0)[None, None])


def solution(mesh):
    placed = (
        P("users", "items", None, None),
        P("users", "items", None),
        P("users", "items"),
        P("users", "items"),
        P("users", "items", None),
        P("users", "items", None, None),
        P("users", "items", None, None),
    )
    return jax.shard_map(
        local,
        mesh=mesh,
        in_specs=placed,
        out_specs=(P("users", "items", None, None), P("users", "items", None, None)),
        check_vma=False,
    )
```

```python
import functools

import jax
import jax.numpy as jnp
from jax import lax
from jax.experimental import pallas as pl
from jax.experimental.pallas import tpu as pltpu
from jax.sharding import PartitionSpec as P


learn_rate = 0.01
shrink_rate = 0.05

LANES = 128
LIVE = 256
VMEM_LIMIT = 16 * 1024 * 1024
CHUNKS = 4
GROUPS = ((3,), (13, 15), (11, 7), (5, 9), (4, 8), (12, 2), (10, 6, 14, 1, 0))

F32 = jnp.float32
BF16 = jnp.bfloat16


def slot_for(owner, slot_owner, count, slots):
    found = jnp.int32(0)
    for slot in range(slots - 1, -1, -1):
        hit = (slot_owner[slot] == owner) & (slot < count)
        found = jnp.where(hit, jnp.int32(slot), found)
    return found


def dot(a, b, ca, cb):
    return lax.dot_general(a, b, (((ca,), (cb,)), ((), ())), preferred_element_type=F32)


def one_hot_rows(code, rows):
    lane_code = jnp.broadcast_to(code, (rows, code.shape[1]))
    row = lax.broadcasted_iota(jnp.int32, lane_code.shape, 0).astype(F32)
    return jnp.where(lane_code == row, 1.0, 0.0).astype(BF16)


def compact_kernel(group, slots, meta_ref, *refs):
    tiles = refs[: len(group)]
    marks_ref = refs[len(group)]
    outs = refs[-len(group) :]
    width = marks_ref.shape[2]
    blocks = width // LANES
    below = lax.broadcasted_iota(jnp.int32, (width, width), 0)
    upto = lax.broadcasted_iota(jnp.int32, (width, width), 1)
    ramp = jnp.where(below <= upto, 1.0, 0.0).astype(BF16)
    me = meta_ref[slots + 1]
    for place, shift in enumerate(group):
        slot = slot_for(lax.rem(me + shift, slots), meta_ref, meta_ref[slots], slots)
        marks = marks_ref[slot].astype(F32)
        marks8 = jnp.broadcast_to(marks, (8, width))
        order = dot(marks8.astype(BF16), ramp, 1, 0)
        code8 = jnp.where(marks8 > 0.5, order - 1.0, -1.0)
        select = one_hot_rows(code8[0:1], LIVE)
        packed = dot(select, tiles[place][0, 0], 1, 0).astype(BF16)
        sub = lax.broadcasted_iota(jnp.int32, (8, LANES), 0)
        tail = jnp.zeros((8, LANES), F32)
        for b in range(blocks):
            lanes = slice(b * LANES, (b + 1) * LANES)
            outs[place][b * LIVE : (b + 1) * LIVE, :] = packed[:, lanes]
            tail = jnp.where(sub == b, code8[:, lanes], tail)
        outs[place][blocks * LIVE :, :] = tail.astype(BF16)


def compact(logs, row_marks, meta, group, slots, after):
    width = logs.shape[2]
    rows = (width // LANES) * LIVE + 8

    def tile_map(shift):
        def index(step, meta_ref):
            owner = lax.rem(meta_ref[slots + 1] + shift, slots)
            return (slot_for(owner, meta_ref, meta_ref[slots], slots), 0, 0, 0)

        return index

    return pl.pallas_call(
        lambda *refs: compact_kernel(group, slots, *refs),
        out_shape=[jax.ShapeDtypeStruct((rows, LANES), BF16) for _ in group],
        grid_spec=pltpu.PrefetchScalarGridSpec(
            num_scalar_prefetch=1,
            grid=(1,),
            in_specs=[pl.BlockSpec((1, 1, width, width), tile_map(shift)) for shift in group]
            + [pl.BlockSpec(row_marks.shape, lambda step, meta_ref: (0, 0, 0))]
            + [pl.BlockSpec(memory_space=pl.ANY)] * len(after),
            out_specs=[pl.BlockSpec((rows, LANES), lambda step, meta_ref: (0, 0)) for _ in group],
        ),
        cost_estimate=pl.CostEstimate(
            flops=len(group) * 2 * LIVE * width * width,
            bytes_accessed=len(group) * 3 * width * width,
            transcendentals=0,
        ),
        compiler_params=pltpu.CompilerParams(vmem_limit_bytes=VMEM_LIMIT),
        name="compact",
    )(meta, *([logs] * len(group)), row_marks, *after)


def stage_kernel(shifts, slots, strata, picked, meta_ref, *refs):
    blocks = refs[: len(shifts)]
    out_ref = refs[len(shifts)]
    sem = refs[len(shifts) + 1]
    me = meta_ref[strata]
    for at, s in enumerate(picked):
        shift = lax.rem(me - meta_ref[s] + slots, slots)
        for place, d in enumerate(shifts):

            @pl.when(shift == d)
            def _():
                pltpu.make_async_copy(blocks[place], out_ref.at[at], sem.at[at]).start()

    for at in range(len(picked)):
        pltpu.make_async_copy(blocks[0], out_ref.at[at], sem.at[at]).wait()


def stage(blocks, shifts, meta, slots, strata, picked):
    rows, lanes = blocks[0].shape
    return pl.pallas_call(
        lambda *refs: stage_kernel(shifts, slots, strata, picked, *refs),
        out_shape=pltpu.VMEM((len(picked), rows, lanes), BF16),
        in_specs=[pl.BlockSpec(memory_space=pltpu.SMEM)]
        + [pl.BlockSpec(memory_space=pl.ANY)] * len(blocks),
        out_specs=pl.BlockSpec(memory_space=pltpu.VMEM),
        scratch_shapes=[pltpu.SemaphoreType.DMA((len(picked),))],
        compiler_params=pltpu.CompilerParams(vmem_limit_bytes=VMEM_LIMIT),
        name="stage",
    )(meta, *blocks)


def code_row(staged_ref, stratum, blocks):
    code = staged_ref[stratum, blocks * LIVE :, :].astype(F32)
    return jnp.concatenate([code[b : b + 1] for b in range(blocks)], axis=1)


def chunk_step(users_live, ratings, items_old):
    predicted = dot(users_live, items_old, 1, 1)
    residual = (ratings.astype(F32) - predicted).astype(BF16)
    item_grad = dot(residual, users_live, 0, 0)
    wide = items_old.astype(F32)
    items_new = wide + learn_rate * (item_grad - shrink_rate * wide)
    return residual, items_new.astype(BF16)


def finish_users(users_old, residuals, items_old, select):
    residual = jnp.concatenate([r[...] for r in residuals], axis=1)
    spread = dot(select, residual, 0, 0).astype(BF16)
    grad = None
    step = spread.shape[1] // len(items_old)
    for k, chunk in enumerate(items_old):
        part = dot(spread[:, k * step : (k + 1) * step], chunk[...], 1, 0)
        grad = part if grad is None else grad + part
    wide = users_old.astype(F32)
    return (wide + learn_rate * (grad - shrink_rate * wide)).astype(BF16)


def ratings_of(staged_ref, stratum, chunk, per):
    first = chunk * per
    parts = [staged_ref[stratum, b * LIVE : (b + 1) * LIVE, :] for b in range(first, first + per)]
    return jnp.concatenate(parts, axis=1)


def live_rows(users, staged_ref, place, live_ref, select_ref):
    select = one_hot_rows(code_row(staged_ref, place, users.shape[0] // LANES), LIVE)
    select_ref[...] = select
    live_ref[...] = dot(select, users, 1, 0).astype(BF16)


def begin_kernel(staged_ref, users_ref, live_ref, select_ref):
    live_rows(users_ref[...], staged_ref, 0, live_ref, select_ref)


def users_kernel(place, chunks, staged_ref, users_ref, select_ref, *refs):
    residuals, items_before = refs[:chunks], refs[chunks : 2 * chunks]
    live_out, select_out, users_out = refs[2 * chunks :]
    users = finish_users(users_ref[...], residuals, items_before, select_ref[...])
    users_out[...] = users
    live_rows(users, staged_ref, place, live_out, select_out)


def next_kernel(stratum, chunk, per, staged_ref, live_ref, items_ref, residual_ref, out_ref):
    ratings = ratings_of(staged_ref, stratum, chunk, per)
    residual, items_new = chunk_step(live_ref[...], ratings, items_ref[...])
    residual_ref[...] = residual
    out_ref[...] = items_new


def last_kernel(chunks, users_ref, select_ref, *refs):
    residuals = refs[:chunks]
    items_before = refs[chunks : 2 * chunks]
    refs[2 * chunks][...] = finish_users(
        users_ref[...], residuals, items_before, select_ref[...]
    )


def run(kernel, operands, outs, flops, name):
    moved = sum(x.size * x.dtype.itemsize for x in outs) * 2
    vmem = pl.BlockSpec(memory_space=pltpu.VMEM)
    return pl.pallas_call(
        kernel,
        out_shape=[pltpu.VMEM(x.shape, x.dtype) for x in outs],
        in_specs=[vmem] * len(operands),
        out_specs=[vmem] * len(outs),
        cost_estimate=pl.CostEstimate(flops=flops, bytes_accessed=moved, transcendentals=0),
        compiler_params=pltpu.CompilerParams(vmem_limit_bytes=VMEM_LIMIT),
        name=name,
    )(*[pltpu.with_memory_space_constraint(x, pltpu.VMEM) for x in operands])


def passed_along(array, axis, by):
    peers = lax.axis_size(axis)
    return lax.ppermute(array, axis, [(i, (i + by) % peers) for i in range(peers)])


def local(logs, tile_rows, slot_owner, counts, owner_source, user_factors, item_factors):
    slots = logs.shape[0]
    strata = owner_source.shape[2]
    me = lax.axis_index("users").astype(jnp.int32)
    meta_out = jnp.concatenate([slot_owner[:, 0], counts[0], me[None]])
    meta_in = jnp.concatenate([owner_source[0, 0], me[None]])

    logs = pltpu.with_memory_space_constraint(logs, pltpu.HBM)
    marks = pltpu.with_memory_space_constraint(tile_rows, pltpu.HBM)
    arrived, shifts, packed = [], [], []
    for group in GROUPS:
        packed = compact(logs, marks, meta_out, group, slots, packed[:1])
        for shift, block in zip(group, packed):
            shifts.append(shift)
            arrived.append(passed_along(block, "users", shift) if shift else block)
    shifts = tuple(shifts)
    early = stage(arrived, shifts, meta_in, slots, strata, (0,))
    late = stage(arrived, shifts, meta_in, slots, strata, tuple(range(1, strata)))

    users = user_factors[0, 0]
    rows, rank = users.shape
    size = rows // CHUNKS
    per = size // LANES
    items = [item_factors[0, 0, k * size : (k + 1) * size] for k in range(CHUNKS)]
    live_shape = jax.ShapeDtypeStruct((LIVE, rank), BF16)
    residual_shape = jax.ShapeDtypeStruct((LIVE, size), BF16)
    chunk_shape = jax.ShapeDtypeStruct((size, rank), BF16)
    users_shape = jax.ShapeDtypeStruct((rows, rank), BF16)
    chunk_flops = 4 * LIVE * size * rank
    users_flops = 2 * rows * rows * (LIVE + rank)

    select_shape = jax.ShapeDtypeStruct((LIVE, rows), BF16)
    live, select = run(
        begin_kernel, [early, users], [live_shape, select_shape], 2 * LIVE * rows * rank, "begin"
    )
    for stratum in range(strata):
        residuals, outgoing, before = [], [], items
        staged, place = (late, stratum - 1) if stratum else (early, 0)
        by = 1 if stratum + 1 < strata else 1 - strata
        for k in range(CHUNKS):
            residual, moved = run(
                functools.partial(next_kernel, place, k, per),
                [staged, live, items[k]],
                [residual_shape, chunk_shape],
                chunk_flops,
                "next",
            )
            residuals.append(residual)
            outgoing.append(passed_along(moved, "items", by))
        items = outgoing
        if stratum + 1 < strata:
            live, select, users = run(
                functools.partial(users_kernel, stratum, CHUNKS),
                [late, users, select] + residuals + before,
                [live_shape, select_shape, users_shape],
                users_flops,
                "users",
            )
    (users,) = run(
        functools.partial(last_kernel, CHUNKS),
        [users, select] + residuals + before,
        [users_shape],
        users_flops,
        "last",
    )
    return (users[None, None], jnp.concatenate(items, axis=0)[None, None])


def solution(mesh):
    placed = (
        P("users", "items", None, None),
        P("users", "items", None),
        P("users", "items"),
        P("users", "items"),
        P("users", "items", None),
        P("users", "items", None, None),
        P("users", "items", None, None),
    )
    return jax.shard_map(
        local,
        mesh=mesh,
        in_specs=placed,
        out_specs=(P("users", "items", None, None), P("users", "items", None, None)),
        check_vma=False,
    )
```
